32 devices in a mesh: row: 4 (over z), col: 8 (over y, x, core).
Axes of the slice: x: 2, y: 2, z: 4, core: 2. Of those that a mesh axis runs over, the one named last changes fastest.
Arguments:
- unfolding: bfloat16 [3072, 4096], P('row', 'col'), may hold values from -400 to 400
Outputs:
- regrouped: bfloat16 [256, 16, 3072], P('col', None, 'row')
The draws below stay inside these ranges and needn't reach their ends.
All inputs are finite; a program needn't handle non-finite values.
Results may differ from the reference program's by a relative error of at most 0.0062.
Values may be sent and summed in bfloat16 or wider, within the bound.
A program may use at most 64 MiB of HBM per device.

```python
import math
import jax
import jax.numpy as jnp

VIEWS = 16
PIXELS = 256
ITERS = 2
ROWS_DEV = 768
COLS = 4096
ROWS = 3072


def draw_unfolding(key, part):
    keys = jax.random.split(jax.random.fold_in(key, 11), 7)
    block_count = ROWS // ROWS_DEV
    block_order = jax.random.permutation(keys[3], block_count).astype(jnp.float32) / max(block_count - 1, 1)
    view_order = jax.random.permutation(keys[4], VIEWS).astype(jnp.float32) / max(VIEWS - 1, 1)
    row_block = block_order[jnp.arange(ROWS) // ROWS_DEV]
    col_block = view_order[jnp.arange(COLS) // PIXELS]
    row_scale = 3.0 ** row_block * jnp.exp(jax.random.uniform(keys[1], (ROWS,), jnp.float32) * math.log(10.0 / 3.0))
    spike_rank = 16
    shrink = min(1.0, ROWS / COLS)
    targets = [shrink * (0.4 + 1.0 * step / (spike_rank - 1)) for step in range(spike_rank)]
    denominator = COLS - 9.0 * sum(targets)
    left_vectors = jax.random.normal(keys[5], (ROWS, spike_rank), jnp.float32)
    right_vectors = jax.random.normal(keys[6], (COLS, spike_rank), jnp.float32)
    spikes = jnp.zeros((ROWS, COLS), jnp.float32)
    for step in range(spike_rank):
        amplitude = math.sqrt(9.0 * targets[step] / denominator)
        spikes = spikes + (amplitude * left_vectors[:, step])[:, None] * right_vectors[:, step][None, :]
    base = jax.random.normal(keys[0], (ROWS, COLS), jnp.float32)
    col_scale = 3.0 ** col_block * jnp.exp(jax.random.uniform(keys[2], (COLS,), jnp.float32) * math.log(10.0 / 3.0))
    inner = jnp.clip(base + spikes, -4.0, 4.0)
    return (inner * row_scale[:, None] * col_scale[None, :]).astype(jnp.bfloat16)


def setup_inputs(seed: int = 0) -> dict:
    key_list = jax.random.split(jax.random.key(seed), 2)
    return {
        "unfolding": draw_unfolding(jax.random.fold_in(key_list[1], 71), 0),
    }


def reference(unfolding):
    values = unfolding.astype(jnp.float32)
    sumsq = jnp.sum(values * values)
    current = (values * (math.sqrt(COLS) / (3.0 * jnp.sqrt(sumsq)))).astype(jnp.bfloat16)
    updated = current.astype(jnp.float32)
    for turn_index in range(ITERS):
        gram = jnp.dot(current.T, current, preferred_element_type=jnp.float32).astype(jnp.bfloat16)
        first = jnp.dot(current, gram, preferred_element_type=jnp.float32).astype(jnp.bfloat16)
        second = jnp.dot(first, gram, preferred_element_type=jnp.float32)
        updated = 1.875 * current.astype(jnp.float32) - 1.25 * first.astype(jnp.float32) + 0.375 * second
        if turn_index + 1 < ITERS:
            current = updated.astype(jnp.bfloat16)
    final = updated * math.sqrt(ROWS)
    cube = final.reshape(ROWS, VIEWS, PIXELS).transpose(2, 1, 0)
    return cube.astype(jnp.bfloat16)
```

```python
import functools
import math

import jax
import jax.numpy as jnp
from jax import lax
from jax.experimental import pallas as pl
from jax.experimental.pallas import tpu as pltpu
from jax.sharding import PartitionSpec as P

PIXELS = 256
ITERS = 2
COLS = 4096
MESH = pl.DeviceIdType.MESH


def exchange(nr, nc, x_ref, out_ref, h_ref, xg, part, sendb, recvb, ssg, full, floats, halves, acc, turned,
             own_sem, a_s, a_r, b_s, b_r, d_s, d_r, s_s, s_r, f_s, f_r, g_s, g_r, x_s, x_r, o_s, o_r):
    r = lax.axis_index("row")
    c = lax.axis_index("col")
    rd = x_ref.shape[0]
    w = x_ref.shape[1] // nr
    st = part.shape[0]
    ch = st // nr

    barrier = pltpu.get_barrier_semaphore()
    for k in range(nr):
        for m in range(nc):
            if k or m:
                pl.semaphore_signal(
                    barrier, inc=1, device_id=(lax.rem(r + k, nr), lax.rem(c + m, nc)), device_id_type=MESH)
    pl.semaphore_wait(barrier, nr * nc - 1)

    def lanes(index):
        return pl.ds(pl.multiple_of(index * w, w), w)

    def rows(index, size):
        return pl.ds(pl.multiple_of(index * size, size), size)

    def to_row(src, dst, s_sem, r_sem, k):
        return pltpu.make_async_remote_copy(
            src_ref=src, dst_ref=dst, send_sem=s_sem, recv_sem=r_sem,
            device_id=(lax.rem(r + k, nr), c), device_id_type=MESH)

    def to_col(src, dst, s_sem, r_sem, d):
        return pltpu.make_async_remote_copy(
            src_ref=src, dst_ref=dst, send_sem=s_sem, recv_sem=r_sem,
            device_id=(r, c ^ d), device_id_type=MESH)

    def gather_col(view, s_sem, r_sem, ready, landed):
        copies = {}

        def send(k, piece, slot, d, part=None):
            ref = view(k, piece)
            if part is not None:
                size = ref.shape[0] // 2
                ref = ref.at[pl.ds(part * size, size), :]
            copies[k, slot] = to_col(ref, ref, s_sem.at[k, slot], r_sem.at[k, slot], d)
            copies[k, slot].start()

        def relay(k):
            copies[k, 2].wait_recv()
            send(k, c ^ 2, 6, 4, 0)
            send(k, c ^ 2, 3, 1)
            copies[k, 4].wait_recv()
            send(k, c ^ 4, 0, 2, 1)
            send(k, c ^ 4, 5, 1)

        def relay_far(k):
            copies[k, 6].wait_recv()
            copies[k, 0].wait_recv()
            send(k, c ^ 6, 7, 1)

        for k in range(nr):
            ready(k)
            for d in (2, 4, 1):
                send(k, c, d, d)
            if k:
                relay(k - 1)
            if k > 1:
                relay_far(k - 2)
        relay(nr - 1)
        for k in range(max(nr - 2, 0), nr):
            relay_far(k)
        for d in (0, 2, 4, 6, 1, 3, 5, 7):
            if d % 2:
                for k in range(nr):
                    copies[k, d].wait_recv()
            landed(c ^ d)
        for key in copies:
            copies[key].wait_send()

    a = {}
    for k in range(1, nr):
        a[k] = to_row(x_ref.at[:, lanes(lax.rem(r + k, nr))], xg.at[rows(r, rd), lanes(c)],
                      a_s.at[k], a_r.at[k], k)
        a[k].start()
    own = pltpu.make_async_copy(x_ref.at[:, lanes(r)], xg.at[rows(r, rd), lanes(c)], own_sem)
    own.start()

    def ready_x(k):
        if k == 0:
            own.wait()
        else:
            a[k].wait_recv()

    gather_col(lambda k, piece: xg.at[rows(lax.rem(r + nr - k, nr), rd), lanes(piece)],
               b_s, b_r, ready_x, lambda piece: None)
    for k in range(1, nr):
        a[k].wait_send()

    left = xg[rows(c, st), :]
    for j in range(nc // 2 + 1):
        right = xg[rows(lax.rem(c + j, nc), st), :]
        block = lax.dot_general(left, right, (((1,), (1,)), ((), ())), preferred_element_type=jnp.float32)
        part[:, j * st:(j + 1) * st] = block
        sendb[:, j * st:(j + 1) * st] = block.astype(jnp.bfloat16)

    dc = {}
    for k in range(1, nr):
        dc[k] = to_row(sendb.at[rows(lax.rem(r + k, nr), ch), :], recvb.at[k - 1], d_s.at[k], d_r.at[k], k)
        dc[k].start()

    step = 32

    def body(i, acc):
        v = xg[rows(i, step), :].astype(jnp.float32)
        v = v * v
        t = acc
        for m in range(step // 8):
            for n in range(v.shape[1] // 128):
                t = t + v[8 * m:8 * m + 8, 128 * n:128 * n + 128]
        return t

    ssg[0] = lax.fori_loop(0, xg.shape[0] // step, body, jnp.zeros((8, 128), jnp.float32))
    sc = {}
    for k in range(1, nr):
        sc[k] = to_row(ssg.at[0], ssg.at[k], s_s.at[k], s_r.at[k], k)
        sc[k].start()
    for k in range(1, nr):
        dc[k].wait_recv()
    total = part[rows(r, ch), :]
    for k in range(1, nr):
        total = total + recvb[k - 1].astype(jnp.float32)
    h_ref[rows(c * nr + r, ch), :] = total.astype(jnp.bfloat16)

    fc = {}
    for k in range(1, nr):
        mine = h_ref.at[rows(c * nr + r, ch), :]
        fc[k] = to_row(mine, mine, f_s.at[k], f_r.at[k], k)
        fc[k].start()

    def ready_h(k):
        if k > 0:
            fc[k].wait_recv()

    half = nc // 2
    core = lax.rem(c, 2)
    first = c - core
    hr = full.shape[0]
    mine_from = core * half

    def mirror(i):
        def turn(index, carry):
            d, t = index // (st // 128), lax.rem(index, st // 128)
            j = lax.rem(i + d, nc)

            @pl.when(j // half == core)
            def _():
                piece = h_ref[pl.ds(pl.multiple_of(i * st + t * 128, 128), 128), lanes_of(d * st, st)]
                full[rows(j - mine_from, st), lanes_of(i * st + t * 128, 128)] = piece.T

            return carry

        def keep(d, carry):
            full[rows(i - mine_from, st), lanes_of(lax.rem(i + d, nc) * st, st)] = (
                h_ref[rows(i, st), lanes_of(d * st, st)])
            return carry

        @pl.when(i // half == core)
        def _():
            lax.fori_loop(0, half + 1, keep, 0)

        lax.fori_loop(st // 128, half * (st // 128), turn, 0)

    def lanes_of(start, size):
        return pl.ds(pl.multiple_of(start, 128), size)

    gather_col(lambda k, piece: h_ref.at[rows(piece * nr + lax.rem(r + nr - k, nr), ch), :],
               g_s, g_r, ready_h, mirror)
    for k in range(1, nr):
        sc[k].wait_recv()
    tot = ssg[0]
    for k in range(1, nr):
        tot = tot + ssg[k]
    for k in range(1, nr):
        dc[k].wait_send()
        sc[k].wait_send()
        fc[k].wait_send()

    sumsq = jnp.full((8, 2 * w), jnp.sum(tot), jnp.float32)
    factor = (math.sqrt(w * nr * nc) / (3.0 * jnp.sqrt(sumsq)))[0:1, :]
    square = factor * factor

    tm = hr // 2
    mine = pl.ds(pl.multiple_of(core * hr, 128), hr)
    theirs = pl.ds(pl.multiple_of((1 - core) * hr, 128), hr)

    def swap(slot, m):
        at = pl.ds(m * tm, tm)
        return pltpu.make_async_remote_copy(
            src_ref=halves.at[slot, 0, at, :], dst_ref=halves.at[slot, 1, at, :],
            send_sem=x_s.at[slot, m], recv_sem=x_r.at[slot, m],
            device_id=(r, c + 1 - 2 * core), device_id_type=MESH)

    def product(slot, emit, number, more=None):
        new = 1 - slot
        for m in range(2):
            at = pl.ds(m * tm, tm)
            acc[at, :] = jnp.dot(full[at, mine], halves[slot, 0], preferred_element_type=jnp.float32)
        for m in range(2):
            if number > 1:
                swap(slot, m).wait_recv()
            if number > 2:
                swap(new, m).wait_send()
        for m in range(2):
            at = pl.ds(m * tm, tm)
            value = square * (acc[at, :] + jnp.dot(
                full[at, theirs], halves[slot, 1], preferred_element_type=jnp.float32))
            value = emit(at, value)
            halves[new, 0, at, :] = value.astype(jnp.bfloat16)
            if more is None:
                swap(new, m).start()
            else:
                pl.when(more)(lambda m=m: swap(new, m).start())

    def store(slot):
        def emit(at, value):
            floats[slot, at, :] = value
            return value
        return emit

    def combine(src, temp, dst):
        def emit(at, two):
            return store(dst)(at, 1.875 * floats[src, at, :] - 1.25 * floats[temp, at, :] + 0.375 * two)
        return emit

    pair = pl.ds(pl.multiple_of(first * w, 128), 2 * w)
    step = tm // 8

    def begin(m, carry):
        at = pl.ds(pl.multiple_of(m * step, step), step)
        value = factor * xg[pl.ds(pl.multiple_of(core * hr + m * step, step), step), pair].astype(jnp.float32)
        floats[0, at, :] = value
        halves[0, 0, at, :] = value.astype(jnp.bfloat16)
        other = factor * xg[pl.ds(pl.multiple_of((1 - core) * hr + m * step, step), step), pair].astype(jnp.float32)
        halves[0, 1, at, :] = other.astype(jnp.bfloat16)
        return carry

    lax.fori_loop(0, hr // step, begin, 0)
    product(0, store(1), 1)
    product(1, combine(0, 1, 2), 2)

    def follow(m, carry):
        at = pl.ds(pl.multiple_of(m * step, step), step)
        floats[4, at, :] = 1.875 * floats[2, at, :]
        return carry

    lax.fori_loop(0, hr // step, follow, 0)

    def level(turn_index, carry):
        weight = jnp.where(turn_index == 0, -1.25, 0.375)

        def inner(k, carry):
            product(turn_index, store(1), 3)
            product(1 - turn_index, combine(2, 1, 2), 3)
            return carry

        lax.fori_loop(0, 2, inner, 0)

        def emit(at, value):
            floats[2, at, :] = value
            floats[4, at, :] += weight * value
            return value

        product(turn_index, emit, 3, turn_index == 0)
        return carry

    lax.fori_loop(0, 2, level, 0)
    for m in range(2):
        swap(1, m).wait_send()

    scale = math.sqrt(xg.shape[0])
    planes = hr // rd

    def flip(m, carry):
        piece = (scale * floats[4, pl.ds(pl.multiple_of(m * 128, 128), 128), :]).T
        turned[m // (rd // 128), :, lanes_of(lax.rem(m, rd // 128) * 128, 128)] = piece.astype(jnp.bfloat16)
        return carry

    lax.fori_loop(0, hr // 128, flip, 0)

    qd = PIXELS // nc
    share = w // qd
    copies = []
    for e in range(2):
        first_col = ((first + e) * nr + r) * w
        view = first_col // PIXELS
        base = lax.rem(first_col, PIXELS) // qd
        for k in range(planes):
            for t in range(share):
                to = core * planes + k
                src = turned.at[k, pl.ds(e * w + t * qd, qd), :]
                dst = out_ref.at[view]
                copy = pltpu.make_async_remote_copy(
                    src_ref=src, dst_ref=dst, send_sem=o_s.at[(e * planes + k) * share + t], recv_sem=o_r.at[view],
                    device_id=(to, base + t), device_id_type=MESH)
                other = jnp.logical_or(base + t != c, to != r)

                @pl.when(other)
                def _(copy=copy):
                    copy.start()

                @pl.when(jnp.logical_not(other))
                def _(src=src, dst=dst):
                    kept = pltpu.make_async_copy(src, dst, own_sem)
                    kept.start()
                    kept.wait()

                copies.append((other, copy))
    for v in range(out_ref.shape[0]):
        group = (v * PIXELS + (c * qd // w) * w) // w
        column = group // nr
        source = (column - lax.rem(column, 2) + r // planes) * nr + lax.rem(group, nr)

        @pl.when(source != c * nr + r)
        def _(v=v):
            pltpu.make_async_remote_copy(
                src_ref=turned.at[0, pl.ds(0, qd), :], dst_ref=out_ref.at[v], send_sem=o_s.at[0],
                recv_sem=o_r.at[v], device_id=(lax.rem(r + 1, nr), c), device_id_type=MESH).wait_recv()
    for other, copy in copies:
        pl.when(other)(lambda copy=copy: copy.wait_send())


def local_rows(unfolding, nr, nc):
    rd, cd = unfolding.shape
    total_rows = rd * nr
    w = cd // nr
    st = total_rows // nc
    half = (nc // 2 + 1) * st
    views = cd * nc // PIXELS
    vm = pl.BlockSpec(memory_space=pltpu.VMEM)
    dma = pltpu.SemaphoreType.DMA
    blocks = pl.pallas_call(
        functools.partial(exchange, nr, nc),
        out_shape=jax.ShapeDtypeStruct((views, PIXELS // nc, rd), jnp.bfloat16),
        in_specs=[vm],
        out_specs=vm,
        scratch_shapes=[
            pltpu.VMEM((total_rows, half), jnp.bfloat16),
            pltpu.VMEM((total_rows, nc * w), jnp.bfloat16),
            pltpu.VMEM((st, half), jnp.float32),
            pltpu.VMEM((st, half), jnp.bfloat16),
            pltpu.VMEM((nr - 1, st // nr, half), jnp.bfloat16),
            pltpu.VMEM((nr, 8, 128), jnp.float32),
            pltpu.VMEM((total_rows // 2, total_rows), jnp.bfloat16),
            pltpu.VMEM((5, total_rows // 2, 2 * w), jnp.float32),
            pltpu.VMEM((2, 2, total_rows // 2, 2 * w), jnp.bfloat16),
            pltpu.VMEM((total_rows // 2, 2 * w), jnp.float32),
            pltpu.VMEM((nr // 2, 2 * w, rd), jnp.bfloat16),
            dma, dma((nr,)), dma((nr,)), dma((nr, nc)), dma((nr, nc)),
            dma((nr,)), dma((nr,)), dma((nr,)), dma((nr,)),
            dma((nr,)), dma((nr,)), dma((nr, nc)), dma((nr, nc)),
            dma((2, 2)), dma((2, 2)), dma((nr * nc,)), dma((views,)),
        ],
        compiler_params=pltpu.CompilerParams(
            collective_id=0, has_side_effects=True, vmem_limit_bytes=63 * 1024 * 1024),
    )(unfolding)
    return blocks.transpose(1, 0, 2)


def local_cols(unfolding):
    rows_dev = unfolding.shape[0]
    cols_dev = unfolding.shape[1]
    total_rows = rows_dev * lax.axis_size("row")
    values = unfolding.astype(jnp.float32)
    sumsq = lax.psum(jnp.sum(values * values), ("row", "col"))
    factor = math.sqrt(COLS) / (3.0 * jnp.sqrt(sumsq))
    current = (values * factor).astype(jnp.bfloat16)
    updated = current.astype(jnp.float32)
    for turn_index in range(ITERS):
        gathered = lax.all_gather(current, "col", axis=1, tiled=True)
        partial_gram = lax.dot_general(
            current, gathered, (((0,), (0,)), ((), ())), preferred_element_type=jnp.float32
        )
        shares = lax.psum_scatter(partial_gram, "row", scatter_dimension=1, tiled=True).astype(
            jnp.bfloat16
        )
        gram_rows = lax.all_gather(shares, "row", axis=1, tiled=True)
        first = lax.dot_general(
            gathered, gram_rows, (((1,), (1,)), ((), ())), preferred_element_type=jnp.float32
        ).astype(jnp.bfloat16)
        second = lax.dot_general(
            lax.all_gather(first, "col", axis=1, tiled=True),
            gram_rows,
            (((1,), (1,)), ((), ())),
            preferred_element_type=jnp.float32,
        )
        updated = (
            1.875 * current.astype(jnp.float32) - 1.25 * first.astype(jnp.float32) + 0.375 * second
        )
        if turn_index + 1 < ITERS:
            current = updated.astype(jnp.bfloat16)
    final = updated * math.sqrt(total_rows)
    view_count = cols_dev // PIXELS
    cube = final.reshape(rows_dev, view_count, PIXELS).transpose(2, 1, 0).astype(jnp.bfloat16)
    return lax.all_to_all(cube, "col", split_axis=0, concat_axis=1, tiled=True)


def solution(mesh):
    nr, nc = mesh.shape["row"], mesh.shape["col"]

    def local(unfolding):
        rd, cd = unfolding.shape
        w = cd // nr
        fits = w == 128 and cd % (128 * nr) == 0 and nc == 8 and rd % 32 == 0 and (rd * nr) % (128 * nc) == 0 and (rd // nc) % 32 == 0
        fits = fits and PIXELS % w == 0 and nr % 2 == 0 and w % (PIXELS // nc) == 0 and rd % 128 == 0 and ITERS == 2
        if rd * nr <= cd * nc and fits:
            return local_rows(unfolding, nr, nc)
        return local_cols(unfolding)

    return jax.shard_map(
        local,
        mesh=mesh,
        in_specs=(P("row", "col"),),
        out_specs=P("col", None, "row"),
        check_vma=False,
    )
```

```python
import functools
import math

import jax
import jax.numpy as jnp
from jax import lax
from jax.experimental import pallas as pl
from jax.experimental.pallas import tpu as pltpu
from jax.sharding import PartitionSpec as P

PIXELS = 256
ITERS = 2
COLS = 4096
MESH = pl.DeviceIdType.MESH


def exchange(nr, nc, x_ref, out_ref, h_ref, xg, part, sendb, recvb, ssg, full, floats, halves, acc, turned,
             own_sem, a_s, a_r, b_s, b_r, d_s, d_r, s_s, s_r, f_s, f_r, g_s, g_r, x_s, x_r, o_s, o_r):
    r = lax.axis_index("row")
    c = lax.axis_index("col")
    rd = x_ref.shape[0]
    w = x_ref.shape[1] // nr
    st = part.shape[0]
    ch = st // nr

    barrier = pltpu.get_barrier_semaphore()
    for k in range(nr):
        for m in range(nc):
            if k or m:
                pl.semaphore_signal(
                    barrier, inc=1, device_id=(lax.rem(r + k, nr), lax.rem(c + m, nc)), device_id_type=MESH)
    pl.semaphore_wait(barrier, nr * nc - 1)

    def lanes(index):
        return pl.ds(pl.multiple_of(index * w, w), w)

    def rows(index, size):
        return pl.ds(pl.multiple_of(index * size, size), size)

    def to_row(src, dst, s_sem, r_sem, k):
        return pltpu.make_async_remote_copy(
            src_ref=src, dst_ref=dst, send_sem=s_sem, recv_sem=r_sem,
            device_id=(lax.rem(r + k, nr), c), device_id_type=MESH)

    def to_col(src, dst, s_sem, r_sem, d):
        return pltpu.make_async_remote_copy(
            src_ref=src, dst_ref=dst, send_sem=s_sem, recv_sem=r_sem,
            device_id=(r, c ^ d), device_id_type=MESH)

    def by_distance(k):
        plane = None
        for at in range(nr):
            choice = sorted(range(nr), key=lambda p: (abs(p - at), p))[k]
            plane = choice if plane is None else jnp.where(r == at, choice, plane)
        return plane

    order = [by_distance(k) for k in range(nr)]

    def to_plane(src, dst, s_sem, r_sem, plane):
        return pltpu.make_async_remote_copy(
            src_ref=src, dst_ref=dst, send_sem=s_sem, recv_sem=r_sem,
            device_id=(plane, c), device_id_type=MESH)

    def gather_col(count, lag, view, s_sem, r_sem, ready, landed):
        copies = {}

        def send(k, piece, slot, d, part=None):
            ref = view(k, piece)
            if part is not None:
                size = ref.shape[0] // 2
                ref = ref.at[pl.ds(part * size, size), :]
            copies[k, slot] = to_col(ref, ref, s_sem.at[k, slot], r_sem.at[k, slot], d)
            copies[k, slot].start()

        def relay(k):
            copies[k, 2].wait_recv()
            send(k, c ^ 2, 6, 4, 0)
            send(k, c ^ 2, 3, 1)
            copies[k, 4].wait_recv()
            send(k, c ^ 4, 0, 2, 1)
            send(k, c ^ 4, 5, 1)

        def relay_far(k):
            copies[k, 6].wait_recv()
            copies[k, 0].wait_recv()
            send(k, c ^ 6, 7, 1)

        for k in range(count):
            ready(k)
            for d in (2, 4, 1):
                send(k, c, d, d)
            if k >= lag:
                relay(k - lag)
            if k >= 2 * lag:
                relay_far(k - 2 * lag)
        for k in range(count - lag, count):
            relay(k)
        for k in range(count - 2 * lag, count):
            relay_far(k)
        for d in (0, 2, 4, 6, 1, 3, 5, 7):
            if d % 2:
                for k in range(count):
                    copies[k, d].wait_recv()
            landed(c ^ d)
        for key in copies:
            copies[key].wait_send()

    ahead = [lax.rem(r + k, nr) for k in range(nr)]
    behind = [lax.rem(r + nr - k, nr) for k in range(nr)]

    def spread(k):
        return to_plane(x_ref.at[:, lanes(ahead[k])], xg.at[rows(r, rd), lanes(c)],
                        a_s.at[k], a_r.at[k], ahead[k])

    for k in range(1, nr):
        spread(k).start()
    own = pltpu.make_async_copy(x_ref.at[:, lanes(r)], xg.at[rows(r, rd), lanes(c)], own_sem)
    own.start()

    def ready_x(k):
        if k == 0:
            own.wait()
        else:
            spread(k).wait_recv()

    gather_col(nr, 1, lambda k, piece: xg.at[rows(behind[k], rd), lanes(piece)],
               b_s, b_r, ready_x, lambda piece: None)
    for k in range(1, nr):
        spread(k).wait_send()

    groups = nc // 2 + 1

    def columns(g):
        return pl.ds(g * st, st)

    def block(g):
        left = xg[rows(c, st), :]
        right = xg[rows(lax.rem(c + g, nc), st), :]
        value = lax.dot_general(left, right, (((1,), (1,)), ((), ())), preferred_element_type=jnp.float32)
        part[:, g * st:(g + 1) * st] = value
        sendb[:, g * st:(g + 1) * st] = value.astype(jnp.bfloat16)

    def scatter(g, k):
        return to_plane(sendb.at[rows(ahead[k], ch), columns(g)], recvb.at[k - 1, :, columns(g)],
                        d_s.at[k, g], d_r.at[k, g], ahead[k])

    def issue(g):
        if g < groups:
            for k in range(1, nr):
                scatter(g, k).start()

    def hop(g, k, up):
        mine = h_ref.at[rows(c * nr + order[k], ch), columns(g)]
        return to_plane(mine, mine, f_s.at[0 if up else 1, k, g], f_r.at[order[k], g], r + 1 if up else r - 1)

    def hops(g, k, act):
        if k == 0:
            pl.when(r < nr - 1)(lambda: act(hop(g, k, True)))
            pl.when(r > 0)(lambda: act(hop(g, k, False)))
        else:
            pl.when(jnp.logical_and(order[k] < r, r < nr - 1))(lambda: act(hop(g, k, True)))
            pl.when(jnp.logical_and(order[k] > r, r > 0))(lambda: act(hop(g, k, False)))

    done = []

    def ready_h(q):
        while len(done) <= min(1 * q, q + 0, groups * nr - 1):
            advance(*divmod(len(done), nr))
            done.append(q)

    def advance(g, k):
        if k == 0:
            total = part[rows(r, ch), g * st:(g + 1) * st]
            for m in range(1, nr):
                scatter(g, m).wait_recv()
                total = total + recvb[m - 1, :, g * st:(g + 1) * st].astype(jnp.float32)
            h_ref[rows(c * nr + r, ch), g * st:(g + 1) * st] = total.astype(jnp.bfloat16)
        else:
            hop(g, k, True).wait_recv()
        hops(g, k, lambda copy: copy.start())
        if k == 0:
            issue(g + 2)

    for g in range(groups):
        block(g)
        if g < 2:
            issue(g)

    step = 32

    def body(i, acc):
        v = xg[rows(i, step), :].astype(jnp.float32)
        v = v * v
        t = acc
        for m in range(step // 8):
            for n in range(v.shape[1] // 128):
                t = t + v[8 * m:8 * m + 8, 128 * n:128 * n + 128]
        return t

    ssg[0] = lax.fori_loop(0, xg.shape[0] // step, body, jnp.zeros((8, 128), jnp.float32))
    sc = {}
    for k in range(1, nr):
        sc[k] = to_row(ssg.at[0], ssg.at[k], s_s.at[k], s_r.at[k], k)
        sc[k].start()

    half = nc // 2
    core = lax.rem(c, 2)
    first = c - core
    hr = full.shape[0]
    mine_from = core * half

    def mirror(i):
        def turn(index, carry):
            d, t = index // (st // 128), lax.rem(index, st // 128)
            j = lax.rem(i + d, nc)

            @pl.when(j // half == core)
            def _():
                piece = h_ref[pl.ds(pl.multiple_of(i * st + t * 128, 128), 128), lanes_of(d * st, st)]
                full[rows(j - mine_from, st), lanes_of(i * st + t * 128, 128)] = piece.T

            return carry

        def keep(d, carry):
            full[rows(i - mine_from, st), lanes_of(lax.rem(i + d, nc) * st, st)] = (
                h_ref[rows(i, st), lanes_of(d * st, st)])
            return carry

        @pl.when(i // half == core)
        def _():
            lax.fori_loop(0, half + 1, keep, 0)

        lax.fori_loop(st // 128, half * (st // 128), turn, 0)

    def lanes_of(start, size):
        return pl.ds(pl.multiple_of(start, 128), size)

    gather_col(groups * nr, 2, lambda q, piece: h_ref.at[rows(piece * nr + order[q % nr], ch), columns(q // nr)],
               g_s, g_r, ready_h, mirror)
    for k in range(1, nr):
        sc[k].wait_recv()
    tot = ssg[0]
    for k in range(1, nr):
        tot = tot + ssg[k]
    for k in range(1, nr):
        sc[k].wait_send()
    for g in range(groups):
        for k in range(nr):
            if k:
                scatter(g, k).wait_send()
            hops(g, k, lambda copy: copy.wait_send())

    sumsq = jnp.full((8, 2 * w), jnp.sum(tot), jnp.float32)
    factor = (math.sqrt(w * nr * nc) / (3.0 * jnp.sqrt(sumsq)))[0:1, :]
    square = factor * factor

    tm = hr // 2
    mine = pl.ds(pl.multiple_of(core * hr, 128), hr)
    theirs = pl.ds(pl.multiple_of((1 - core) * hr, 128), hr)

    def swap(slot, m):
        at = pl.ds(m * tm, tm)
        return pltpu.make_async_remote_copy(
            src_ref=halves.at[slot, 0, at, :], dst_ref=halves.at[slot, 1, at, :],
            send_sem=x_s.at[slot, m], recv_sem=x_r.at[slot, m],
            device_id=(r, c + 1 - 2 * core), device_id_type=MESH)

    def product(slot, emit, number, more=None):
        new = 1 - slot
        for m in range(2):
            at = pl.ds(m * tm, tm)
            acc[at, :] = jnp.dot(full[at, mine], halves[slot, 0], preferred_element_type=jnp.float32)
        for m in range(2):
            if number > 1:
                swap(slot, m).wait_recv()
            if number > 2:
                swap(new, m).wait_send()
        for m in range(2):
            at = pl.ds(m * tm, tm)
            value = square * (acc[at, :] + jnp.dot(
                full[at, theirs], halves[slot, 1], preferred_element_type=jnp.float32))
            value = emit(at, value)
            halves[new, 0, at, :] = value.astype(jnp.bfloat16)
            if more is None:
                swap(new, m).start()
            else:
                pl.when(more)(lambda m=m: swap(new, m).start())

    def store(slot):
        def emit(at, value):
            floats[slot, at, :] = value
            return value
        return emit

    def combine(src, temp, dst):
        def emit(at, two):
            return store(dst)(at, 1.875 * floats[src, at, :] - 1.25 * floats[temp, at, :] + 0.375 * two)
        return emit

    pair = pl.ds(pl.multiple_of(first * w, 128), 2 * w)
    step = tm // 8

    def begin(m, carry):
        at = pl.ds(pl.multiple_of(m * step, step), step)
        value = factor * xg[pl.ds(pl.multiple_of(core * hr + m * step, step), step), pair].astype(jnp.float32)
        floats[0, at, :] = value
        halves[0, 0, at, :] = value.astype(jnp.bfloat16)
        other = factor * xg[pl.ds(pl.multiple_of((1 - core) * hr + m * step, step), step), pair].astype(jnp.float32)
        halves[0, 1, at, :] = other.astype(jnp.bfloat16)
        return carry

    lax.fori_loop(0, hr // step, begin, 0)
    product(0, store(1), 1)
    product(1, combine(0, 1, 2), 2)

    def follow(m, carry):
        at = pl.ds(pl.multiple_of(m * step, step), step)
        floats[4, at, :] = 1.875 * floats[2, at, :]
        return carry

    lax.fori_loop(0, hr // step, follow, 0)

    def level(turn_index, carry):
        weight = jnp.where(turn_index == 0, -1.25, 0.375)

        def inner(k, carry):
            product(turn_index, store(1), 3)
            product(1 - turn_index, combine(2, 1, 2), 3)
            return carry

        lax.fori_loop(0, 2, inner, 0)

        def emit(at, value):
            floats[2, at, :] = value
            floats[4, at, :] += weight * value
            return value

        product(turn_index, emit, 3, turn_index == 0)
        return carry

    lax.fori_loop(0, 2, level, 0)
    for m in range(2):
        swap(1, m).wait_send()

    scale = math.sqrt(xg.shape[0])
    planes = hr // rd

    def flip(m, carry):
        piece = (scale * floats[4, pl.ds(pl.multiple_of(m * 128, 128), 128), :]).T
        turned[m // (rd // 128), :, lanes_of(lax.rem(m, rd // 128) * 128, 128)] = piece.astype(jnp.bfloat16)
        return carry

    lax.fori_loop(0, hr // 128, flip, 0)

    qd = PIXELS // nc
    share = w // qd
    copies = []
    for e in range(2):
        first_col = ((first + e) * nr + r) * w
        view = first_col // PIXELS
        base = lax.rem(first_col, PIXELS) // qd
        for k in range(planes):
            for t in range(share):
                to = core * planes + k
                src = turned.at[k, pl.ds(e * w + t * qd, qd), :]
                dst = out_ref.at[view]
                copy = pltpu.make_async_remote_copy(
                    src_ref=src, dst_ref=dst, send_sem=o_s.at[(e * planes + k) * share + t], recv_sem=o_r.at[view],
                    device_id=(to, base + t), device_id_type=MESH)
                other = jnp.logical_or(base + t != c, to != r)

                @pl.when(other)
                def _(copy=copy):
                    copy.start()

                @pl.when(jnp.logical_not(other))
                def _(src=src, dst=dst):
                    kept = pltpu.make_async_copy(src, dst, own_sem)
                    kept.start()
                    kept.wait()

                copies.append((other, copy))
    for v in range(out_ref.shape[0]):
        group = (v * PIXELS + (c * qd // w) * w) // w
        column = group // nr
        source = (column - lax.rem(column, 2) + r // planes) * nr + lax.rem(group, nr)

        @pl.when(source != c * nr + r)
        def _(v=v):
            pltpu.make_async_remote_copy(
                src_ref=turned.at[0, pl.ds(0, qd), :], dst_ref=out_ref.at[v], send_sem=o_s.at[0],
                recv_sem=o_r.at[v], device_id=(lax.rem(r + 1, nr), c), device_id_type=MESH).wait_recv()
    for other, copy in copies:
        pl.when(other)(lambda copy=copy: copy.wait_send())


def local_rows(unfolding, nr, nc):
    rd, cd = unfolding.shape
    total_rows = rd * nr
    w = cd // nr
    st = total_rows // nc
    groups = nc // 2 + 1
    half = groups * st
    views = cd * nc // PIXELS
    vm = pl.BlockSpec(memory_space=pltpu.VMEM)
    dma = pltpu.SemaphoreType.DMA
    blocks = pl.pallas_call(
        functools.partial(exchange, nr, nc),
        out_shape=jax.ShapeDtypeStruct((views, PIXELS // nc, rd), jnp.bfloat16),
        in_specs=[vm],
        out_specs=vm,
        scratch_shapes=[
            pltpu.VMEM((total_rows, half), jnp.bfloat16),
            pltpu.VMEM((total_rows, nc * w), jnp.bfloat16),
            pltpu.VMEM((st, half), jnp.float32),
            pltpu.VMEM((st, half), jnp.bfloat16),
            pltpu.VMEM((nr - 1, st // nr, half), jnp.bfloat16),
            pltpu.VMEM((nr, 8, 128), jnp.float32),
            pltpu.VMEM((total_rows // 2, total_rows), jnp.bfloat16),
            pltpu.VMEM((5, total_rows // 2, 2 * w), jnp.float32),
            pltpu.VMEM((2, 2, total_rows // 2, 2 * w), jnp.bfloat16),
            pltpu.VMEM((total_rows // 2, 2 * w), jnp.float32),
            pltpu.VMEM((nr // 2, 2 * w, rd), jnp.bfloat16),
            dma, dma((nr,)), dma((nr,)), dma((nr, nc)), dma((nr, nc)),
            dma((nr, groups)), dma((nr, groups)), dma((nr,)), dma((nr,)),
            dma((2, nr, groups)), dma((nr, groups)), dma((groups * nr, nc)), dma((groups * nr, nc)),
            dma((2, 2)), dma((2, 2)), dma((nr * nc,)), dma((views,)),
        ],
        compiler_params=pltpu.CompilerParams(
            collective_id=0, has_side_effects=True, vmem_limit_bytes=63 * 1024 * 1024),
    )(unfolding)
    return blocks.transpose(1, 0, 2)


def local_cols(unfolding):
    rows_dev = unfolding.shape[0]
    cols_dev = unfolding.shape[1]
    total_rows = rows_dev * lax.axis_size("row")
    values = unfolding.astype(jnp.float32)
    sumsq = lax.psum(jnp.sum(values * values), ("row", "col"))
    factor = math.sqrt(COLS) / (3.0 * jnp.sqrt(sumsq))
    current = (values * factor).astype(jnp.bfloat16)
    updated = current.astype(jnp.float32)
    for turn_index in range(ITERS):
        gathered = lax.all_gather(current, "col", axis=1, tiled=True)
        partial_gram = lax.dot_general(
            current, gathered, (((0,), (0,)), ((), ())), preferred_element_type=jnp.float32
        )
        shares = lax.psum_scatter(partial_gram, "row", scatter_dimension=1, tiled=True).astype(
            jnp.bfloat16
        )
        gram_rows = lax.all_gather(shares, "row", axis=1, tiled=True)
        first = lax.dot_general(
            gathered, gram_rows, (((1,), (1,)), ((), ())), preferred_element_type=jnp.float32
        ).astype(jnp.bfloat16)
        second = lax.dot_general(
            lax.all_gather(first, "col", axis=1, tiled=True),
            gram_rows,
            (((1,), (1,)), ((), ())),
            preferred_element_type=jnp.float32,
        )
        updated = (
            1.875 * current.astype(jnp.float32) - 1.25 * first.astype(jnp.float32) + 0.375 * second
        )
        if turn_index + 1 < ITERS:
            current = updated.astype(jnp.bfloat16)
    final = updated * math.sqrt(total_rows)
    view_count = cols_dev // PIXELS
    cube = final.reshape(rows_dev, view_count, PIXELS).transpose(2, 1, 0).astype(jnp.bfloat16)
    return lax.all_to_all(cube, "col", split_axis=0, concat_axis=1, tiled=True)


def solution(mesh):
    nr, nc = mesh.shape["row"], mesh.shape["col"]

    def local(unfolding):
        rd, cd = unfolding.shape
        w = cd // nr
        fits = w == 128 and cd % (128 * nr) == 0 and nc == 8 and rd % 32 == 0 and (rd * nr) % (128 * nc) == 0 and (rd // nc) % 32 == 0
        fits = fits and PIXELS % w == 0 and nr % 2 == 0 and w % (PIXELS // nc) == 0 and rd % 128 == 0 and ITERS == 2
        if rd * nr <= cd * nc and fits:
            return local_rows(unfolding, nr, nc)
        return local_cols(unfolding)

    return jax.shard_map(
        local,
        mesh=mesh,
        in_specs=(P("row", "col"),),
        out_specs=P("col", None, "row"),
        check_vma=False,
    )
```

```python
import functools
import math

import jax
import jax.numpy as jnp
from jax import lax
from jax.experimental import pallas as pl
from jax.experimental.pallas import tpu as pltpu
from jax.sharding import PartitionSpec as P

PIXELS = 256
ITERS = 2
COLS = 4096
MESH = pl.DeviceIdType.MESH


def exchange(nr, nc, x_ref, out_ref, h_ref, xg, part, sendb, recvb, ssg, full, floats, halves, acc, turned,
             own_sem, a_s, a_r, b_s, b_r, d_s, d_r, s_s, s_r, f_s, f_r, g_s, g_r, x_s, x_r, o_s, o_r):
    r = lax.axis_index("row")
    c = lax.axis_index("col")
    rd = x_ref.shape[0]
    w = x_ref.shape[1] // nr
    st = part.shape[0]
    ch = st // nr

    barrier = pltpu.get_barrier_semaphore()
    for k in range(nr):
        for m in range(nc):
            if k or m:
                pl.semaphore_signal(
                    barrier, inc=1, device_id=(lax.rem(r + k, nr), lax.rem(c + m, nc)), device_id_type=MESH)
    pl.semaphore_wait(barrier, nr * nc - 1)

    def lanes(index):
        return pl.ds(pl.multiple_of(index * w, w), w)

    def rows(index, size):
        return pl.ds(pl.multiple_of(index * size, size), size)

    def to_row(src, dst, s_sem, r_sem, k):
        return pltpu.make_async_remote_copy(
            src_ref=src, dst_ref=dst, send_sem=s_sem, recv_sem=r_sem,
            device_id=(lax.rem(r + k, nr), c), device_id_type=MESH)

    def to_col(src, dst, s_sem, r_sem, d):
        return pltpu.make_async_remote_copy(
            src_ref=src, dst_ref=dst, send_sem=s_sem, recv_sem=r_sem,
            device_id=(r, c ^ d), device_id_type=MESH)

    def by_distance(k):
        plane = None
        for at in range(nr):
            choice = sorted(range(nr), key=lambda p: (abs(p - at), p))[k]
            plane = choice if plane is None else jnp.where(r == at, choice, plane)
        return plane

    order = [by_distance(k) for k in range(nr)]

    def to_plane(src, dst, s_sem, r_sem, plane):
        return pltpu.make_async_remote_copy(
            src_ref=src, dst_ref=dst, send_sem=s_sem, recv_sem=r_sem,
            device_id=(plane, c), device_id_type=MESH)

    def gather_col(count, lag, view, s_sem, r_sem, ready, landed):
        copies = {}

        def send(k, piece, slot, d, part=None):
            ref = view(k, piece)
            if part is not None:
                size = ref.shape[0] // 32 * 16
                ref = ref.at[pl.ds(part * size, ref.shape[0] - size if part else size), :]
            copies[k, slot] = to_col(ref, ref, s_sem.at[k, slot], r_sem.at[k, slot], d)
            copies[k, slot].start()

        def relay(k):
            copies[k, 2].wait_recv()
            send(k, c ^ 2, 6, 4, 0)
            send(k, c ^ 2, 3, 1)
            copies[k, 4].wait_recv()
            send(k, c ^ 4, 0, 2, 1)
            send(k, c ^ 4, 5, 1)

        def relay_far(k):
            copies[k, 6].wait_recv()
            copies[k, 0].wait_recv()
            send(k, c ^ 6, 7, 1)

        for k in range(count):
            ready(k)
            for d in (2, 4, 1):
                send(k, c, d, d)
            if k >= lag:
                relay(k - lag)
            if k >= 2 * lag:
                relay_far(k - 2 * lag)
        for k in range(count - lag, count):
            relay(k)
        for k in range(count - 2 * lag, count):
            relay_far(k)
        for d in (0, 2, 4, 6, 1, 3, 5, 7):
            if d % 2:
                for k in range(count):
                    copies[k, d].wait_recv()
            landed(c ^ d)
        for key in copies:
            copies[key].wait_send()

    ahead = [lax.rem(r + k, nr) for k in range(nr)]
    behind = [lax.rem(r + nr - k, nr) for k in range(nr)]

    def spread(k):
        return to_plane(x_ref.at[:, lanes(ahead[k])], xg.at[rows(r, rd), lanes(c)],
                        a_s.at[k], a_r.at[k], ahead[k])

    for k in range(1, nr):
        spread(k).start()
    own = pltpu.make_async_copy(x_ref.at[:, lanes(r)], xg.at[rows(r, rd), lanes(c)], own_sem)
    own.start()

    def ready_x(k):
        if k == 0:
            own.wait()
        else:
            spread(k).wait_recv()

    gather_col(nr, 1, lambda k, piece: xg.at[rows(behind[k], rd), lanes(piece)],
               b_s, b_r, ready_x, lambda piece: None)
    for k in range(1, nr):
        spread(k).wait_send()

    groups = nc // 2 + 1

    def columns(g):
        return pl.ds(g * st, st)

    def height(g):
        return ch if g < groups - 1 else ch // 2

    def chunk(g, piece, plane):
        return pl.ds(pl.multiple_of(piece * st + plane * height(g), 16), height(g))

    def block(g):
        if g < groups - 1:
            left = xg[rows(c, st), :]
            right = xg[rows(lax.rem(c + g, nc), st), :]
        else:
            left = xg[rows(lax.rem(c, nc // 2) * 2 + c // (nc // 2), st // 2), :]
            right = xg[rows(lax.rem(c, nc // 2) + nc // 2, st), :]
        value = lax.dot_general(left, right, (((1,), (1,)), ((), ())), preferred_element_type=jnp.float32)
        part[0:nr * height(g), g * st:(g + 1) * st] = value
        sendb[0:nr * height(g), g * st:(g + 1) * st] = value.astype(jnp.bfloat16)

    def scatter(g, k):
        return to_plane(sendb.at[rows(ahead[k], height(g)), columns(g)], recvb.at[k - 1, pl.ds(0, height(g)), columns(g)],
                        d_s.at[k, g], d_r.at[k, g], ahead[k])

    def issue(g):
        if g < groups:
            for k in range(1, nr):
                scatter(g, k).start()

    def hop(g, k, up):
        mine = h_ref.at[chunk(g, c, order[k]), columns(g)]
        return to_plane(mine, mine, f_s.at[0 if up else 1, k, g], f_r.at[order[k], g], r + 1 if up else r - 1)

    def hops(g, k, act):
        if k == 0:
            pl.when(r < nr - 1)(lambda: act(hop(g, k, True)))
            pl.when(r > 0)(lambda: act(hop(g, k, False)))
        else:
            pl.when(jnp.logical_and(order[k] < r, r < nr - 1))(lambda: act(hop(g, k, True)))
            pl.when(jnp.logical_and(order[k] > r, r > 0))(lambda: act(hop(g, k, False)))

    items = sorted(((g, k) for g in range(groups) for k in range(nr)), key=lambda i: (2 * i[0] + i[1], i[0]))

    def ready_h(q):
        advance(*items[q])

    def advance(g, k):
        if k == 0:
            total = part[rows(r, height(g)), g * st:(g + 1) * st]
            for m in range(1, nr):
                scatter(g, m).wait_recv()
                total = total + recvb[m - 1, 0:height(g), g * st:(g + 1) * st].astype(jnp.float32)
            h_ref[chunk(g, c, r), g * st:(g + 1) * st] = total.astype(jnp.bfloat16)
        else:
            hop(g, k, True).wait_recv()
        hops(g, k, lambda copy: copy.start())
        if k == 0:
            issue(g + 2)

    for g in range(groups):
        block(g)
        if g < 2:
            issue(g)

    step = 32

    def body(i, acc):
        v = xg[rows(i, step), :].astype(jnp.float32)
        v = v * v
        t = acc
        for m in range(step // 8):
            for n in range(v.shape[1] // 128):
                t = t + v[8 * m:8 * m + 8, 128 * n:128 * n + 128]
        return t

    ssg[0] = lax.fori_loop(0, xg.shape[0] // step, body, jnp.zeros((8, 128), jnp.float32))
    sc = {}
    for k in range(1, nr):
        sc[k] = to_row(ssg.at[0], ssg.at[k], s_s.at[k], s_r.at[k], k)
        sc[k].start()

    half = nc // 2
    core = lax.rem(c, 2)
    first = c - core
    hr = full.shape[0]
    mine_from = core * half

    def mirror(i):
        def turn(index, carry):
            d, t = index // (st // 128), lax.rem(index, st // 128)
            j = lax.rem(i + d, nc)

            @pl.when(j // half == core)
            def _():
                piece = h_ref[pl.ds(pl.multiple_of(i * st + t * 128, 128), 128), lanes_of(d * st, st)]
                full[rows(j - mine_from, st), lanes_of(i * st + t * 128, 128)] = piece.T

            return carry

        def keep(d, carry):
            full[rows(i - mine_from, st), lanes_of(lax.rem(i + d, nc) * st, st)] = (
                h_ref[rows(i, st), lanes_of(d * st, st)])
            return carry

        @pl.when(i // half == core)
        def _():
            lax.fori_loop(0, half, keep, 0)

        lax.fori_loop(st // 128, half * (st // 128), turn, 0)

    def lanes_of(start, size):
        return pl.ds(pl.multiple_of(start, 128), size)

    gather_col(groups * nr, 2, lambda q, piece: h_ref.at[chunk(items[q][0], piece, order[items[q][1]]), columns(items[q][0])],
               g_s, g_r, ready_h, mirror)

    def across(a, carry):
        low, high, hs = a * st, (a + half) * st, st // 2
        cols = pl.ds(half * st, st)

        def take(start, size):
            return h_ref[pl.ds(pl.multiple_of(start, 16), size), cols]

        @pl.when(core == 0)
        def _():
            full[pl.ds(pl.multiple_of(low, 16), hs), lanes_of(high, st)] = take(low, hs)
            full[pl.ds(pl.multiple_of(low + hs, 16), hs), lanes_of(high, st)] = take(high, hs)

        @pl.when(core == 1)
        def _():
            for t in range(st // 128):
                start, stop = t * 128, t * 128 + 128
                if stop <= hs:
                    piece = take(low + start, 128)
                elif start >= hs:
                    piece = take(high + start - hs, 128)
                else:
                    piece = jnp.concatenate([take(low + start, hs - start), take(high, stop - hs)], axis=0)
                full[rows(a, st), lanes_of(low + start, 128)] = piece.T

        return carry

    lax.fori_loop(0, half, across, 0)
    for k in range(1, nr):
        sc[k].wait_recv()
    tot = ssg[0]
    for k in range(1, nr):
        tot = tot + ssg[k]
    for k in range(1, nr):
        sc[k].wait_send()
    for g in range(groups):
        for k in range(nr):
            if k:
                scatter(g, k).wait_send()
            hops(g, k, lambda copy: copy.wait_send())

    sumsq = jnp.full((8, 2 * w), jnp.sum(tot), jnp.float32)
    factor = (math.sqrt(w * nr * nc) / (3.0 * jnp.sqrt(sumsq)))[0:1, :]
    square = factor * factor

    tm = hr // 2
    mine = pl.ds(pl.multiple_of(core * hr, 128), hr)
    theirs = pl.ds(pl.multiple_of((1 - core) * hr, 128), hr)

    def swap(slot, m):
        at = pl.ds(m * tm, tm)
        return pltpu.make_async_remote_copy(
            src_ref=halves.at[slot, 0, at, :], dst_ref=halves.at[slot, 1, at, :],
            send_sem=x_s.at[slot, m], recv_sem=x_r.at[slot, m],
            device_id=(r, c + 1 - 2 * core), device_id_type=MESH)

    def product(slot, emit, number, more=None):
        new = 1 - slot
        for m in range(2):
            at = pl.ds(m * tm, tm)
            acc[at, :] = jnp.dot(full[at, mine], halves[slot, 0], preferred_element_type=jnp.float32)
        for m in range(2):
            if number > 1:
                swap(slot, m).wait_recv()
            if number > 2:
                swap(new, m).wait_send()
        for m in range(2):
            at = pl.ds(m * tm, tm)
            value = square * (acc[at, :] + jnp.dot(
                full[at, theirs], halves[slot, 1], preferred_element_type=jnp.float32))
            value = emit(at, value)
            halves[new, 0, at, :] = value.astype(jnp.bfloat16)
            if more is None:
                swap(new, m).start()
            else:
                pl.when(more)(lambda m=m: swap(new, m).start())

    def store(slot):
        def emit(at, value):
            floats[slot, at, :] = value
            return value
        return emit

    def combine(src, temp, dst):
        def emit(at, two):
            return store(dst)(at, 1.875 * floats[src, at, :] - 1.25 * floats[temp, at, :] + 0.375 * two)
        return emit

    pair = pl.ds(pl.multiple_of(first * w, 128), 2 * w)
    step = tm // 8

    def begin(m, carry):
        at = pl.ds(pl.multiple_of(m * step, step), step)
        value = factor * xg[pl.ds(pl.multiple_of(core * hr + m * step, step), step), pair].astype(jnp.float32)
        floats[0, at, :] = value
        halves[0, 0, at, :] = value.astype(jnp.bfloat16)
        other = factor * xg[pl.ds(pl.multiple_of((1 - core) * hr + m * step, step), step), pair].astype(jnp.float32)
        halves[0, 1, at, :] = other.astype(jnp.bfloat16)
        return carry

    lax.fori_loop(0, hr // step, begin, 0)
    product(0, store(1), 1)
    product(1, combine(0, 1, 2), 2)

    def follow(m, carry):
        at = pl.ds(pl.multiple_of(m * step, step), step)
        floats[4, at, :] = 1.875 * floats[2, at, :]
        return carry

    lax.fori_loop(0, hr // step, follow, 0)

    def level(turn_index, carry):
        weight = jnp.where(turn_index == 0, -1.25, 0.375)

        def inner(k, carry):
            product(turn_index, store(1), 3)
            product(1 - turn_index, combine(2, 1, 2), 3)
            return carry

        lax.fori_loop(0, 2, inner, 0)

        def emit(at, value):
            floats[2, at, :] = value
            floats[4, at, :] += weight * value
            return value

        product(turn_index, emit, 3, turn_index == 0)
        return carry

    lax.fori_loop(0, 2, level, 0)
    for m in range(2):
        swap(1, m).wait_send()

    scale = math.sqrt(xg.shape[0])
    planes = hr // rd

    def flip(m, carry):
        piece = (scale * floats[4, pl.ds(pl.multiple_of(m * 128, 128), 128), :]).T
        turned[m // (rd // 128), :, lanes_of(lax.rem(m, rd // 128) * 128, 128)] = piece.astype(jnp.bfloat16)
        return carry

    lax.fori_loop(0, hr // 128, flip, 0)

    qd = PIXELS // nc
    share = w // qd
    copies = []
    for e in range(2):
        first_col = ((first + e) * nr + r) * w
        view = first_col // PIXELS
        base = lax.rem(first_col, PIXELS) // qd
        for k in range(planes):
            for t in range(share):
                to = core * planes + k
                src = turned.at[k, pl.ds(e * w + t * qd, qd), :]
                dst = out_ref.at[view]
                copy = pltpu.make_async_remote_copy(
                    src_ref=src, dst_ref=dst, send_sem=o_s.at[(e * planes + k) * share + t], recv_sem=o_r.at[view],
                    device_id=(to, base + t), device_id_type=MESH)
                other = jnp.logical_or(base + t != c, to != r)

                @pl.when(other)
                def _(copy=copy):
                    copy.start()

                @pl.when(jnp.logical_not(other))
                def _(src=src, dst=dst):
                    kept = pltpu.make_async_copy(src, dst, own_sem)
                    kept.start()
                    kept.wait()

                copies.append((other, copy))
    for v in range(out_ref.shape[0]):
        group = (v * PIXELS + (c * qd // w) * w) // w
        column = group // nr
        source = (column - lax.rem(column, 2) + r // planes) * nr + lax.rem(group, nr)

        @pl.when(source != c * nr + r)
        def _(v=v):
            pltpu.make_async_remote_copy(
                src_ref=turned.at[0, pl.ds(0, qd), :], dst_ref=out_ref.at[v], send_sem=o_s.at[0],
                recv_sem=o_r.at[v], device_id=(lax.rem(r + 1, nr), c), device_id_type=MESH).wait_recv()
    for other, copy in copies:
        pl.when(other)(lambda copy=copy: copy.wait_send())


def local_rows(unfolding, nr, nc):
    rd, cd = unfolding.shape
    total_rows = rd * nr
    w = cd // nr
    st = total_rows // nc
    groups = nc // 2 + 1
    half = groups * st
    views = cd * nc // PIXELS
    vm = pl.BlockSpec(memory_space=pltpu.VMEM)
    dma = pltpu.SemaphoreType.DMA
    blocks = pl.pallas_call(
        functools.partial(exchange, nr, nc),
        out_shape=jax.ShapeDtypeStruct((views, PIXELS // nc, rd), jnp.bfloat16),
        in_specs=[vm],
        out_specs=vm,
        scratch_shapes=[
            pltpu.VMEM((total_rows, half), jnp.bfloat16),
            pltpu.VMEM((total_rows, nc * w), jnp.bfloat16),
            pltpu.VMEM((st, half), jnp.float32),
            pltpu.VMEM((st, half), jnp.bfloat16),
            pltpu.VMEM((nr - 1, st // nr, half), jnp.bfloat16),
            pltpu.VMEM((nr, 8, 128), jnp.float32),
            pltpu.VMEM((total_rows // 2, total_rows), jnp.bfloat16),
            pltpu.VMEM((5, total_rows // 2, 2 * w), jnp.float32),
            pltpu.VMEM((2, 2, total_rows // 2, 2 * w), jnp.bfloat16),
            pltpu.VMEM((total_rows // 2, 2 * w), jnp.float32),
            pltpu.VMEM((nr // 2, 2 * w, rd), jnp.bfloat16),
            dma, dma((nr,)), dma((nr,)), dma((nr, nc)), dma((nr, nc)),
            dma((nr, groups)), dma((nr, groups)), dma((nr,)), dma((nr,)),
            dma((2, nr, groups)), dma((nr, groups)), dma((groups * nr, nc)), dma((groups * nr, nc)),
            dma((2, 2)), dma((2, 2)), dma((nr * nc,)), dma((views,)),
        ],
        compiler_params=pltpu.CompilerParams(
            collective_id=0, has_side_effects=True, vmem_limit_bytes=63 * 1024 * 1024),
    )(unfolding)
    return blocks.transpose(1, 0, 2)


def local_cols(unfolding):
    rows_dev = unfolding.shape[0]
    cols_dev = unfolding.shape[1]
    total_rows = rows_dev * lax.axis_size("row")
    values = unfolding.astype(jnp.float32)
    sumsq = lax.psum(jnp.sum(values * values), ("row", "col"))
    factor = math.sqrt(COLS) / (3.0 * jnp.sqrt(sumsq))
    current = (values * factor).astype(jnp.bfloat16)
    updated = current.astype(jnp.float32)
    for turn_index in range(ITERS):
        gathered = lax.all_gather(current, "col", axis=1, tiled=True)
        partial_gram = lax.dot_general(
            current, gathered, (((0,), (0,)), ((), ())), preferred_element_type=jnp.float32
        )
        shares = lax.psum_scatter(partial_gram, "row", scatter_dimension=1, tiled=True).astype(
            jnp.bfloat16
        )
        gram_rows = lax.all_gather(shares, "row", axis=1, tiled=True)
        first = lax.dot_general(
            gathered, gram_rows, (((1,), (1,)), ((), ())), preferred_element_type=jnp.float32
        ).astype(jnp.bfloat16)
        second = lax.dot_general(
            lax.all_gather(first, "col", axis=1, tiled=True),
            gram_rows,
            (((1,), (1,)), ((), ())),
            preferred_element_type=jnp.float32,
        )
        updated = (
            1.875 * current.astype(jnp.float32) - 1.25 * first.astype(jnp.float32) + 0.375 * second
        )
        if turn_index + 1 < ITERS:
            current = updated.astype(jnp.bfloat16)
    final = updated * math.sqrt(total_rows)
    view_count = cols_dev // PIXELS
    cube = final.reshape(rows_dev, view_count, PIXELS).transpose(2, 1, 0).astype(jnp.bfloat16)
    return lax.all_to_all(cube, "col", split_axis=0, concat_axis=1, tiled=True)


def solution(mesh):
    nr, nc = mesh.shape["row"], mesh.shape["col"]

    def local(unfolding):
        rd, cd = unfolding.shape
        w = cd // nr
        fits = w == 128 and cd % (128 * nr) == 0 and nc == 8 and rd % 32 == 0 and (rd * nr) % (128 * nc) == 0 and (rd // nc) % 32 == 0
        fits = fits and PIXELS % w == 0 and nr % 2 == 0 and w % (PIXELS // nc) == 0 and rd % 128 == 0 and ITERS == 2
        if rd * nr <= cd * nc and fits:
            return local_rows(unfolding, nr, nc)
        return local_cols(unfolding)

    return jax.shard_map(
        local,
        mesh=mesh,
        in_specs=(P("row", "col"),),
        out_specs=P("col", None, "row"),
        check_vma=False,
    )
```
